32 devices in a mesh: vocab: 8 (over y, x, core), hid: 4 (over z).
Axes of the slice: x: 2, y: 2, z: 4, core: 2. Of those that a mesh axis runs over, the one named last changes fastest.
Arguments:
- hidden: bfloat16 [1, 1024, 3584], P(None, 'vocab', 'hid'), may hold values from -30 to 30
- unembed: bfloat16 [3584, 81920], P(None, ('vocab', 'hid')), may hold values from -10 to 10
- labels: int32 [1024], P('vocab'), may hold values from 0 to 81919
Outputs:
- token_loss: float32 [1, 1024], replicated
- layer_loss: float32 [1], replicated
The draws below stay inside these ranges and needn't reach their ends.
All inputs are finite; a program needn't handle non-finite values.
Results may differ from the reference program's by a relative error of at most 0.0003.
Values may be sent and summed in bfloat16 or wider, within the bound.
A program may use at most 128 MiB of HBM per device.

```python
import math
import jax
import jax.numpy as jnp
import numpy as np
from jax import lax

D = 3584
V = 81920
LAYERS = 1
TOK_DEV = 128
TOKENS = 1024


def draw_hidden(key, part):
    values = jnp.clip(jax.random.normal(jax.random.fold_in(key, 1), (LAYERS, TOKENS, D), jnp.float32), -6.0, 6.0)
    return values.astype(jnp.bfloat16)


def draw_unembed(key, part):
    values = jnp.clip(jax.random.normal(jax.random.fold_in(key, 3), (D, V), jnp.float32), -6.0, 6.0)
    values = values * (3.0 / math.sqrt(D))
    return values.astype(jnp.bfloat16)


def set_ends(result, key, smallest, top_value):
    index_at = [jax.random.randint(jax.random.fold_in(key, axis), (), 0, length) for axis, length in enumerate(result.shape)]
    widest = result.shape.index(max(result.shape))
    next_to = index_at[:widest] + [(index_at[widest] + 1) % result.shape[widest]] + index_at[widest + 1:]
    return result.at[tuple(index_at)].set(smallest).at[tuple(next_to)].set(top_value)


def wide_ids(own_key, shape, number_of, skew):
    loads = [min(1 << octave, number_of + 1 - (1 << octave)) * (1 << 20) // math.isqrt((1 << octave) ** skew) + 1 for octave in range((number_of + 1).bit_length()) if 1 << octave <= number_of]
    scale = 1 + sum(loads) // (1 << 30)
    grid = np.cumsum(np.array([max(1, weight // scale) for weight in loads]))
    pick = jax.random.randint(jax.random.fold_in(own_key, 1), shape, 0, int(grid[len(loads) - 1]))
    start = jnp.left_shift(1, jnp.searchsorted(jnp.asarray(grid, jnp.int32), pick, side="right").astype(jnp.int32))
    rank = start - 1 + jax.random.randint(jax.random.fold_in(own_key, 4), shape, 0, 1 << 30) % jnp.minimum(start, number_of + 1 - start)
    return jax.random.permutation(jax.random.fold_in(own_key, 2), number_of)[rank].astype(jnp.int32)


def setup_inputs(seed: int = 0) -> dict:
    splits = jax.random.split(jax.random.key(seed), 4)
    hidden = draw_hidden(jax.random.fold_in(splits[3], 71), 0)
    unembed = draw_unembed(jax.random.fold_in(splits[3], 71), 0)
    labels = set_ends(wide_ids(splits[2], (TOKENS,), V, 2), jax.random.fold_in(splits[2], 3), 0, V - 1).astype(jnp.int32)
    return dict(hidden=hidden, unembed=unembed, labels=labels)


def reference(hidden, unembed, labels):
    token_rows = hidden.reshape(-1, TOK_DEV, D)
    targets = jnp.tile(labels, LAYERS).reshape(-1, TOK_DEV).astype(jnp.int32)

    def one_block(block_pair):
        row_block, wanted = block_pair
        logits = jnp.dot(row_block, unembed, preferred_element_type=jnp.float32)
        row_peak = jnp.max(logits, axis=-1)
        row_total = jnp.sum(jnp.exp(logits - row_peak[:, None]), axis=-1)
        picked = jnp.take_along_axis(logits, wanted[:, None], axis=-1)[:, 0]
        return row_peak + jnp.log(row_total) - picked

    token_loss = lax.map(one_block, (token_rows, targets)).reshape(LAYERS, TOKENS)
    return token_loss, jnp.mean(token_loss, axis=1)
```

```python
import functools

import jax
import jax.numpy as jnp
from jax import lax
from jax.experimental import pallas as pl
from jax.experimental.pallas import tpu as pltpu
from jax.sharding import PartitionSpec as P

MESH = pl.DeviceIdType.MESH
LANES = 128


def bits_of(mask):
    return [1 << b for b in range(mask.bit_length()) if mask >> b & 1]


def parent_dim(group, piece):
    dims = bits_of(group)
    return dims[piece % len(dims)]


def flip(index, mask):
    for bit in bits_of(mask):
        index = index + bit - 2 * bit * lax.rem(index // bit, 2)
    return index


def combine(parts, blocks):
    peaks = [part[0:blocks] for part in parts]
    peak = functools.reduce(jnp.maximum, peaks)
    total = sum(part[blocks : 2 * blocks] * jnp.exp(own - peak) for part, own in zip(parts, peaks))
    picked = sum(part[2 * blocks : 3 * blocks] for part in parts)
    return peak, total, picked


def kernel(
    n_v, n_h, layers,
    hid_hbm, w_hbm, lab_ref,
    loss_ref,
    buf, w, acc, labs, part, rel_stats, line, plane,
    own_sem, w_sem, send_sem, recv_sem, lab_send, lab_recv, line_send, line_recv, plane_send, plane_recv,
):
    v, z = lax.axis_index("vocab"), lax.axis_index("hid")
    rows = hid_hbm.shape[0]
    depth = hid_hbm.shape[1]
    cols = w_hbm.shape[1]
    first_col = (v * n_h + z) * cols
    dims = [1 << b for b in range((n_v // 2).bit_length() - 1)]
    groups = sorted(range(n_v // 2), key=lambda g: (len(bits_of(g)), g))
    pos = {2 * g + c: 2 * i + c for i, g in enumerate(groups) for c in range(2)}
    blocks = n_v * layers

    own = pltpu.make_async_copy(hid_hbm, buf.at[0, pl.ds(0, rows)], own_sem)
    own.start()
    w_copies = []
    for s in range(n_h):
        src = lax.rem(z - s + n_h, n_h)
        copy = pltpu.make_async_copy(
            w_hbm.at[pl.ds(pl.multiple_of(src * depth, depth), depth)], w.at[s], w_sem.at[s]
        )
        w_copies.append(copy)

    barrier = pltpu.get_barrier_semaphore()
    line_peers = [lax.rem(z + j, n_h) for j in range(1, n_h)]
    for peer in line_peers:
        pl.semaphore_signal(barrier, inc=1, device_id=(v, peer), device_id_type=MESH)
    for m in range(1, n_v):
        pl.semaphore_signal(barrier, inc=1, device_id=(flip(v, m), z), device_id_type=MESH)
    for copy in w_copies:
        copy.start()
    pl.semaphore_wait(barrier, n_h + n_v - 2)
    own.wait()

    sends = []

    def block_at(m, s):
        return buf.at[s, pl.ds(pos[m] * rows, rows)]

    def block_copy(m, s, to_m, to_s, device):
        k = len(sends)
        return pltpu.make_async_remote_copy(
            src_ref=block_at(m, s), dst_ref=block_at(to_m, to_s),
            send_sem=send_sem.at[min(k, send_sem.shape[0] - 1)],
            recv_sem=recv_sem.at[to_m * n_h + to_s],
            device_id=device, device_id_type=MESH,
        )

    def send(m, s, to_m, to_s, device):
        copy = block_copy(m, s, to_m, to_s, device)
        copy.start()
        sends.append(copy)

    def wait_block(m, s):
        if (m, s) != (0, 0):
            block_copy(m, s, m, s, (flip(v, 1), z)).wait_recv()

    def to_line(s):
        if s < n_h - 1:
            send(0, s, 0, s + 1, (v, lax.rem(z + 1, n_h)))

    def to_dims(g, s):
        for d in dims:
            if not g & d and parent_dim(g | d, s) == d:
                send(2 * g, s, 2 * (g | d), s, (flip(v, 2 * d), z))

    def to_pair(g, s):
        send(2 * g, s, 2 * g + 1, s, (flip(v, 1), z))

    tile = max(t for t in (512, 384, 256, 128) if cols % t == 0)

    def multiply(first, count, s):
        lo, size = first * 2 * rows, count * 2 * rows
        step = 1024 if size > 1024 and size % 1024 == 0 else size

        @pl.loop(0, cols // tile)
        def _(n):
            at = pl.ds(pl.multiple_of(n * tile, tile), tile)
            for r in range(lo, lo + size, step):
                value = jnp.dot(
                    buf[s, r : r + step, :], w[s, :, at], preferred_element_type=jnp.float32
                )
                if s == 0:
                    acc[r : r + step, at] = value
                else:
                    acc[r : r + step, at] = acc[r : r + step, at] + value

    def stats(first, count):
        half = 64

        @pl.loop(first * 2 * layers, (first + count) * 2 * layers)
        def _(p):
            label = labs[p // layers].astype(jnp.float32)
            label = jnp.transpose(jnp.broadcast_to(label, (LANES, LANES)))
            lane = lax.broadcasted_iota(jnp.int32, (half, LANES), 1) + first_col
            lane = lane.astype(jnp.float32)
            for h in range(LANES // half):
                at = pl.ds(pl.multiple_of(p * LANES + h * half, half), half)
                peak = acc[at, 0:LANES]
                for c in range(LANES, cols, LANES):
                    peak = jnp.maximum(peak, acc[at, c : c + LANES])
                here = slice(h * half, (h + 1) * half)
                part[0, here, :] = peak
                row_peak = jnp.max(peak, axis=1, keepdims=True)
                row_peak = jnp.broadcast_to(row_peak, (half, LANES))
                wanted = label[here] - lane
                total = jnp.zeros((half, LANES), jnp.float32)
                picked = jnp.zeros((half, LANES), jnp.float32)
                for c in range(0, cols, LANES):
                    x = acc[at, c : c + LANES]
                    total = total + jnp.exp(x - row_peak)
                    picked = picked + jnp.where(wanted == float(c), x, 0.0)
                part[1, here, :] = total
                part[2, here, :] = picked
            rel_stats[0, p] = jnp.max(jnp.transpose(part[0]), axis=0, keepdims=True)
            rel_stats[1, p] = jnp.sum(jnp.transpose(part[1]), axis=0, keepdims=True)
            rel_stats[2, p] = jnp.sum(jnp.transpose(part[2]), axis=0, keepdims=True)

    to_line(0)
    to_dims(0, 0)
    to_pair(0, 0)
    lab_copies = []
    for m in range(1, n_v):
        copy = pltpu.make_async_remote_copy(
            src_ref=lab_ref, dst_ref=labs.at[pos[m]],
            send_sem=lab_send.at[m - 1], recv_sem=lab_recv.at[m - 1],
            device_id=(flip(v, m), z), device_id_type=MESH,
        )
        copy.start()
        lab_copies.append(copy)
    labs[0] = lab_ref[...]

    near = [g for g in groups if len(bits_of(g)) == 1]
    far = [g for g in groups if len(bits_of(g)) > 1]
    for s in range(1, n_h + 1):
        if s < n_h:
            wait_block(0, s)
            to_line(s)
            to_dims(0, s)
            to_pair(0, s)
        for g in near:
            wait_block(2 * g, s - 1)
            to_pair(g, s - 1)
        late = range(s) if s == n_h - 1 else ([s - 1] if s == n_h else [])
        for t in late:
            for g in near:
                to_dims(g, t)
        for g in [0] + near:
            wait_block(2 * g + 1, s - 1)
        w_copies[s - 1].wait()
        multiply(0, 1 + len(near), s - 1)
    for copy in lab_copies:
        copy.wait()
    if not far:
        stats(0, 1 + len(near))
    else:
        levels = sorted({len(bits_of(g)) for g in far})
        done = 1 + len(near)
        stats(0, done)
        for level in levels:
            here = [g for g in far if len(bits_of(g)) == level]
            for s in range(n_h):
                for g in here:
                    wait_block(2 * g, s)
                    to_dims(g, s)
                    to_pair(g, s)
            for s in range(n_h):
                for g in here:
                    wait_block(2 * g + 1, s)
                multiply(done, len(here), s)
            stats(done, len(here))
            done += len(here)

    for m in range(n_v):
        for l in range(layers):
            for k in range(3):
                line[z, pl.ds(k * blocks + flip(v, m) * layers + l, 1), :] = rel_stats[k, pos[m] * layers + l]
    line_copies = []
    for j, peer in enumerate(line_peers):
        copy = pltpu.make_async_remote_copy(
            src_ref=line.at[z], dst_ref=line.at[z],
            send_sem=line_send.at[j], recv_sem=line_recv.at[j],
            device_id=(v, peer), device_id_type=MESH,
        )
        copy.start()
        line_copies.append(copy)
    for copy in line_copies:
        copy.wait_recv()
    peak, total, picked = combine([line[h] for h in range(n_h)], blocks)
    plane[v, 0:blocks, :] = peak
    plane[v, blocks : 2 * blocks, :] = total
    plane[v, 2 * blocks : 3 * blocks, :] = picked
    plane_copies = []
    for m in range(1, n_v):
        copy = pltpu.make_async_remote_copy(
            src_ref=plane.at[v], dst_ref=plane.at[v],
            send_sem=plane_send.at[m - 1], recv_sem=plane_recv.at[m - 1],
            device_id=(flip(v, m), z), device_id_type=MESH,
        )
        copy.start()
        plane_copies.append(copy)
    for copy in sends + line_copies:
        copy.wait_send()
    for copy in plane_copies:
        copy.wait_recv()
    peak, total, picked = combine([plane[u] for u in range(n_v)], blocks)
    loss_ref[...] = peak + jnp.log(total) - picked
    for copy in plane_copies:
        copy.wait_send()


def body(hidden, unembed, labels, n_v, n_h):
    layers, tokens, depth = hidden.shape
    cols = unembed.shape[1]
    rows = layers * tokens
    blocks = n_v * layers
    dma = pltpu.SemaphoreType.DMA
    any_space = pl.BlockSpec(memory_space=pl.ANY)
    vmem = pl.BlockSpec(memory_space=pltpu.VMEM)
    loss = pl.pallas_call(
        functools.partial(kernel, n_v, n_h, layers),
        out_shape=jax.ShapeDtypeStruct((blocks, tokens), jnp.float32),
        in_specs=[any_space, any_space, vmem],
        out_specs=vmem,
        scratch_shapes=[
            pltpu.VMEM((n_h, n_v * rows, depth), jnp.bfloat16),
            pltpu.VMEM((n_h, depth, cols), jnp.bfloat16),
            pltpu.VMEM((n_v * rows, cols), jnp.float32),
            pltpu.VMEM((n_v, 1, tokens), jnp.int32),
            pltpu.VMEM((3, LANES, LANES), jnp.float32),
            pltpu.VMEM((3, blocks, 1, tokens), jnp.float32),
            pltpu.VMEM((n_h, 3 * blocks, tokens), jnp.float32),
            pltpu.VMEM((n_v, 3 * blocks, tokens), jnp.float32),
            dma,
            dma((n_h,)),
            dma((n_v * n_h - 1,)),
            dma((n_v * n_h,)),
            dma((n_v - 1,)),
            dma((n_v - 1,)),
            dma((n_h - 1,)),
            dma((n_h - 1,)),
            dma((n_v - 1,)),
            dma((n_v - 1,)),
        ],
        compiler_params=pltpu.CompilerParams(
            collective_id=0, has_side_effects=True, vmem_limit_bytes=60 * 2**20
        ),
    )(hidden.reshape(rows, depth), unembed, labels.reshape(1, tokens))
    token_loss = loss.reshape(n_v, layers, tokens).transpose(1, 0, 2).reshape(layers, n_v * tokens)
    return token_loss, jnp.mean(token_loss, axis=1)


def solution(mesh):
    placed = (P(None, "vocab", "hid"), P(None, ("vocab", "hid")), P("vocab"))
    inner = functools.partial(body, n_v=mesh.shape["vocab"], n_h=mesh.shape["hid"])
    return jax.shard_map(inner, mesh=mesh, in_specs=placed, out_specs=(P(), P()), check_vma=False)
```

```python
import functools

import jax
import jax.numpy as jnp
from jax import lax
from jax.experimental import pallas as pl
from jax.experimental.pallas import tpu as pltpu
from jax.sharding import PartitionSpec as P

MESH = pl.DeviceIdType.MESH
LANES = 128
CUTS = 2


def bits_of(mask):
    return [1 << b for b in range(mask.bit_length()) if mask >> b & 1]


def via_dim(group, piece):
    dims = bits_of(group)
    return dims[piece] if 1 < len(dims) and piece < len(dims) else dims[0] if len(dims) == 1 else None


def arrival(group, s):
    if group == 0:
        return s
    dim = via_dim(group, s)
    if dim is None:
        return 1 + arrival(group, s - 1)
    if group == dim:
        return s + 1 if s < 2 else s + 2
    return max(3, 1 + arrival(group ^ dim, s))


def flip(index, mask):
    for bit in bits_of(mask):
        index = index + bit - 2 * bit * lax.rem(index // bit, 2)
    return index


def combine(parts, blocks):
    peaks = [part[0:blocks] for part in parts]
    peak = functools.reduce(jnp.maximum, peaks)
    total = sum(part[blocks : 2 * blocks] * jnp.exp(own - peak) for part, own in zip(parts, peaks))
    picked = sum(part[2 * blocks : 3 * blocks] for part in parts)
    return peak, total, picked


def kernel(
    n_v, n_h, layers,
    hid_hbm, w_hbm, lab_ref,
    loss_ref, mean_ref,
    buf, w, acc, labs, part, rel_stats, line, plane,
    own_sem, w_sem, send_sem, recv_sem, lab_send, lab_recv, line_send, line_recv, plane_send, plane_recv,
):
    v, z = lax.axis_index("vocab"), lax.axis_index("hid")
    rows = hid_hbm.shape[0]
    depth = hid_hbm.shape[1]
    cols = w_hbm.shape[1]
    first_col = (v * n_h + z) * cols
    dims = [1 << b for b in range((n_v // 2).bit_length() - 1)]
    groups = sorted(range(n_v // 2), key=lambda g: (len(bits_of(g)), g))
    pos = {2 * g + c: 2 * i + c for i, g in enumerate(groups) for c in range(2)}
    blocks = n_v * layers

    own = pltpu.make_async_copy(hid_hbm, buf.at[0, pl.ds(0, rows)], own_sem)
    own.start()
    w_copies = []
    for s in range(n_h):
        src = lax.rem(z - s + n_h, n_h)
        copy = pltpu.make_async_copy(
            w_hbm.at[pl.ds(pl.multiple_of(src * depth, depth), depth)], w.at[s], w_sem.at[s]
        )
        w_copies.append(copy)

    barrier = pltpu.get_barrier_semaphore()
    line_peers = [lax.rem(z + j, n_h) for j in range(1, n_h)]
    for peer in line_peers:
        pl.semaphore_signal(barrier, inc=1, device_id=(v, peer), device_id_type=MESH)
    for m in range(1, n_v):
        pl.semaphore_signal(barrier, inc=1, device_id=(flip(v, m), z), device_id_type=MESH)
    for copy in w_copies:
        copy.start()
    pl.semaphore_wait(barrier, n_h + n_v - 2)
    own.wait()

    cuts = CUTS if n_v * n_h <= 64 else 1
    piece = rows // cuts
    sends = []

    def block_copy(m, s, to_m, to_s, cut, device):
        k = min(len(sends), send_sem.shape[0] - 1)
        return pltpu.make_async_remote_copy(
            src_ref=buf.at[s, pl.ds(pos[m] * rows + cut * piece, piece)],
            dst_ref=buf.at[to_s, pl.ds(pos[to_m] * rows + cut * piece, piece)],
            send_sem=send_sem.at[k],
            recv_sem=recv_sem.at[(to_m * n_h + to_s) * cuts + cut],
            device_id=device, device_id_type=MESH,
        )

    def send(m, s, to_m, to_s, cut, device):
        copy = block_copy(m, s, to_m, to_s, cut, device)
        copy.start()
        sends.append(copy)

    def wait_block(m, s, cut):
        if (m, s) != (0, 0):
            block_copy(m, s, m, s, cut, (flip(v, 1), z)).wait_recv()

    def arrive(g, s, cut):
        wait_block(2 * g, s, cut)
        if s + 1 < n_h and (g == 0 or via_dim(g, s + 1) is None):
            send(2 * g, s, 2 * g, s + 1, cut, (v, lax.rem(z + 1, n_h)))
        for d in dims:
            if not g & d and via_dim(g | d, s) == d:
                send(2 * g, s, 2 * (g | d), s, cut, (flip(v, 2 * d), z))
        send(2 * g, s, 2 * g + 1, s, cut, (flip(v, 1), z))

    tile = max(t for t in (512, 384, 256, 128) if cols % t == 0)

    tiles = cols // tile
    waited = set()

    def multiply(first, count, s, tile_lo, tile_hi):
        if tile_lo == tile_hi:
            return
        for g in groups[first : first + count]:
            for cut in range(cuts):
                if (g, s, cut) not in waited:
                    wait_block(2 * g + 1, s, cut)
                    waited.add((g, s, cut))
        if s not in waited:
            w_copies[s].wait()
            waited.add(s)
        lo, size = first * 2 * rows, count * 2 * rows
        step = 1024 if size > 1024 and size % 1024 == 0 else size

        @pl.loop(tile_lo, tile_hi)
        def _(n):
            at = pl.ds(pl.multiple_of(n * tile, tile), tile)
            for r in range(lo, lo + size, step):
                value = jnp.dot(
                    buf[s, r : r + step, :], w[s, :, at], preferred_element_type=jnp.float32
                )
                if s == 0:
                    acc[r : r + step, at] = value
                else:
                    acc[r : r + step, at] = acc[r : r + step, at] + value

    def stats(first, count):
        half = 64

        @pl.loop(first * 2 * layers, (first + count) * 2 * layers)
        def _(p):
            label = labs[p // layers].astype(jnp.float32)
            label = jnp.transpose(jnp.broadcast_to(label, (LANES, LANES)))
            lane = lax.broadcasted_iota(jnp.int32, (half, LANES), 1) + first_col
            lane = lane.astype(jnp.float32)
            for h in range(LANES // half):
                at = pl.ds(pl.multiple_of(p * LANES + h * half, half), half)
                peak = acc[at, 0:LANES]
                for c in range(LANES, cols, LANES):
                    peak = jnp.maximum(peak, acc[at, c : c + LANES])
                here = slice(h * half, (h + 1) * half)
                part[0, here, :] = peak
                row_peak = jnp.max(peak, axis=1, keepdims=True)
                row_peak = jnp.broadcast_to(row_peak, (half, LANES))
                wanted = label[here] - lane
                total = jnp.zeros((half, LANES), jnp.float32)
                picked = jnp.zeros((half, LANES), jnp.float32)
                for c in range(0, cols, LANES):
                    x = acc[at, c : c + LANES]
                    total = total + jnp.exp(x - row_peak)
                    picked = picked + jnp.where(wanted == float(c), x, 0.0)
                part[1, here, :] = total
                part[2, here, :] = picked
            rel_stats[0, p] = jnp.max(jnp.transpose(part[0]), axis=0, keepdims=True)
            rel_stats[1, p] = jnp.sum(jnp.transpose(part[1]), axis=0, keepdims=True)
            rel_stats[2, p] = jnp.sum(jnp.transpose(part[2]), axis=0, keepdims=True)

    for cut in range(cuts):
        arrive(0, 0, cut)
    lab_copies = []
    for m in range(1, n_v):
        copy = pltpu.make_async_remote_copy(
            src_ref=lab_ref, dst_ref=labs.at[pos[m]],
            send_sem=lab_send.at[m - 1], recv_sem=lab_recv.at[m - 1],
            device_id=(flip(v, m), z), device_id_type=MESH,
        )
        copy.start()
        lab_copies.append(copy)
    labs[0] = lab_ref[...]

    all_blocks = [(g, s) for s in range(n_h) for g in groups]
    last = max(arrival(g, s) for g, s in all_blocks)
    events, jobs = {}, {}
    for t in range(last + 1):
        here = [block for block in all_blocks if arrival(*block) == t]
        events[t] = sorted(here, key=lambda block: (block[0] == 0) == (t == 2))
        ready = [(g, s) for g, s in all_blocks if t == (s + (s > 0) if g == 0 else arrival(g, s))]
        jobs[t] = []
        for g, s in ready:
            i = groups.index(g)
            if jobs[t] and jobs[t][-1][2] == s and sum(jobs[t][-1][:2]) == i:
                first, count, _ = jobs[t].pop()
                jobs[t].append((first, count + 1, s))
            else:
                jobs[t].append((i, 1, s))

    def run(t, lo, hi):
        total = sum(count for _, count, _ in jobs[t]) * tiles
        begin, end, at = total * lo // 3, total * hi // 3, 0
        for first, count, s in jobs[t]:
            first_tile = min(max(0, (begin - at) // count), tiles)
            last_tile = min(max(0, (end - at) // count), tiles)
            multiply(first, count, s, first_tile, last_tile)
            at += count * tiles

    for t in range(last + 1):
        for cut in range(cuts):
            if t > 0:
                for g, s in events[t]:
                    arrive(g, s, cut)
            if t > 1 and cut < cuts - 1:
                run(t - 1, 1, 2)
        if t > 1:
            run(t - 1, 1 if cuts == 1 else 2, 3)
        run(t, 0, 3 if t == 0 or t == last else 1)
        if t == 1 and last == 1:
            run(1, 1, 3)
    for copy in lab_copies:
        copy.wait()
    stats(0, len(groups))

    for m in range(n_v):
        for l in range(layers):
            for k in range(3):
                line[z, pl.ds(k * blocks + flip(v, m) * layers + l, 1), :] = rel_stats[k, pos[m] * layers + l]
    line_copies = []
    for j, peer in enumerate(line_peers):
        copy = pltpu.make_async_remote_copy(
            src_ref=line.at[z], dst_ref=line.at[z],
            send_sem=line_send.at[j], recv_sem=line_recv.at[j],
            device_id=(v, peer), device_id_type=MESH,
        )
        copy.start()
        line_copies.append(copy)
    for copy in line_copies:
        copy.wait_recv()
    peak, total, picked = combine([line[h] for h in range(n_h)], blocks)
    plane[v, 0:blocks, :] = peak
    plane[v, blocks : 2 * blocks, :] = total
    plane[v, 2 * blocks : 3 * blocks, :] = picked
    plane_copies = []
    for m in range(1, n_v):
        copy = pltpu.make_async_remote_copy(
            src_ref=plane.at[v], dst_ref=plane.at[v],
            send_sem=plane_send.at[m - 1], recv_sem=plane_recv.at[m - 1],
            device_id=(flip(v, m), z), device_id_type=MESH,
        )
        copy.start()
        plane_copies.append(copy)
    for copy in sends + line_copies:
        copy.wait_send()
    for copy in plane_copies:
        copy.wait_recv()
    peak, total, picked = combine([plane[u] for u in range(n_v)], blocks)
    loss = peak + jnp.log(total) - picked
    for l in range(layers):
        sums = jnp.zeros((1, LANES), jnp.float32)
        for u in range(n_v):
            row = loss[u * layers + l : u * layers + l + 1]
            loss_ref[l : l + 1, u * LANES : (u + 1) * LANES] = row
            sums = sums + row
        mean_ref[l] = jnp.sum(sums) / (n_v * LANES)
    for copy in plane_copies:
        copy.wait_send()


def body(hidden, unembed, labels, n_v, n_h):
    layers, tokens, depth = hidden.shape
    cols = unembed.shape[1]
    rows = layers * tokens
    blocks = n_v * layers
    dma = pltpu.SemaphoreType.DMA
    any_space = pl.BlockSpec(memory_space=pl.ANY)
    vmem = pl.BlockSpec(memory_space=pltpu.VMEM)
    cuts = CUTS if n_v * n_h <= 64 else 1
    return pl.pallas_call(
        functools.partial(kernel, n_v, n_h, layers),
        out_shape=(
            jax.ShapeDtypeStruct((layers, n_v * tokens), jnp.float32),
            jax.ShapeDtypeStruct((layers,), jnp.float32),
        ),
        in_specs=[any_space, any_space, vmem],
        out_specs=(vmem, pl.BlockSpec(memory_space=pltpu.SMEM)),
        scratch_shapes=[
            pltpu.VMEM((n_h, n_v * rows, depth), jnp.bfloat16),
            pltpu.VMEM((n_h, depth, cols), jnp.bfloat16),
            pltpu.VMEM((n_v * rows, cols), jnp.float32),
            pltpu.VMEM((n_v, 1, tokens), jnp.int32),
            pltpu.VMEM((3, LANES, LANES), jnp.float32),
            pltpu.VMEM((3, blocks, 1, tokens), jnp.float32),
            pltpu.VMEM((n_h, 3 * blocks, tokens), jnp.float32),
            pltpu.VMEM((n_v, 3 * blocks, tokens), jnp.float32),
            dma,
            dma((n_h,)),
            dma(((n_v * n_h - 1) * cuts,)),
            dma((n_v * n_h * cuts,)),
            dma((n_v - 1,)),
            dma((n_v - 1,)),
            dma((n_h - 1,)),
            dma((n_h - 1,)),
            dma((n_v - 1,)),
            dma((n_v - 1,)),
        ],
        compiler_params=pltpu.CompilerParams(
            collective_id=0, has_side_effects=True, vmem_limit_bytes=60 * 2**20
        ),
    )(hidden.reshape(rows, depth), unembed, labels.reshape(1, tokens))


def solution(mesh):
    placed = (P(None, "vocab", "hid"), P(None, ("vocab", "hid")), P("vocab"))
    inner = functools.partial(body, n_v=mesh.shape["vocab"], n_h=mesh.shape["hid"])
    return jax.shard_map(inner, mesh=mesh, in_specs=placed, out_specs=(P(), P()), check_vma=False)
```

```python
import functools

import jax
import jax.numpy as jnp
from jax import lax
from jax.experimental import pallas as pl
from jax.experimental.pallas import tpu as pltpu
from jax.sharding import PartitionSpec as P

MESH = pl.DeviceIdType.MESH
LANES = 128
CUTS = 2


def bits_of(mask):
    return [1 << b for b in range(mask.bit_length()) if mask >> b & 1]


def via_dim(group, piece):
    dims = bits_of(group)
    return dims[piece] if 1 < len(dims) and piece < len(dims) else dims[0] if len(dims) == 1 else None


def arrival(group, s):
    if group == 0:
        return s
    dim = via_dim(group, s)
    if dim is None:
        return 1 + arrival(group, s - 1)
    if group == dim:
        return s + 1 if s < 2 else s + 2
    return max(3, 1 + arrival(group ^ dim, s))


def flip(index, mask):
    for bit in bits_of(mask):
        index = index + bit - 2 * bit * lax.rem(index // bit, 2)
    return index


def combine(parts, blocks):
    peaks = [part[0:blocks] for part in parts]
    peak = functools.reduce(jnp.maximum, peaks)
    total = sum(part[blocks : 2 * blocks] * jnp.exp(own - peak) for part, own in zip(parts, peaks))
    picked = sum(part[2 * blocks : 3 * blocks] for part in parts)
    return peak, total, picked


def kernel(
    n_v, n_h, layers,
    hid_hbm, w_hbm, lab_ref,
    loss_ref, mean_ref,
    buf, w, acc, labs, part, rel_stats, line, plane,
    own_sem, w_sem, send_sem, recv_sem, lab_send, lab_recv, line_send, line_recv, plane_send, plane_recv,
):
    v, z = lax.axis_index("vocab"), lax.axis_index("hid")
    rows = hid_hbm.shape[0]
    depth = hid_hbm.shape[1]
    cols = w_hbm.shape[1]
    first_col = (v * n_h + z) * cols
    dims = [1 << b for b in range((n_v // 2).bit_length() - 1)]
    groups = sorted(range(n_v // 2), key=lambda g: (len(bits_of(g)), g))
    pos = {2 * g + c: 2 * i + c for i, g in enumerate(groups) for c in range(2)}
    blocks = n_v * layers

    own = pltpu.make_async_copy(hid_hbm, buf.at[pl.ds(0, rows), pl.ds(0, depth)], own_sem)
    own.start()
    w_copies = []
    for s in range(n_h):
        src = lax.rem(z - s + n_h, n_h)
        copy = pltpu.make_async_copy(
            w_hbm.at[pl.ds(pl.multiple_of(src * depth, depth), depth)], w.at[pl.ds(s * depth, depth)], w_sem.at[s]
        )
        w_copies.append(copy)

    barrier = pltpu.get_barrier_semaphore()
    line_peers = [lax.rem(z + j, n_h) for j in range(1, n_h)]
    for peer in line_peers:
        pl.semaphore_signal(barrier, inc=1, device_id=(v, peer), device_id_type=MESH)
    for m in range(1, n_v):
        pl.semaphore_signal(barrier, inc=1, device_id=(flip(v, m), z), device_id_type=MESH)
    for copy in w_copies:
        copy.start()
    pl.semaphore_wait(barrier, n_h + n_v - 2)
    own.wait()

    cuts = CUTS if n_v * n_h <= 64 else 1
    piece = rows // cuts
    sends = []

    def block_copy(m, s, to_m, to_s, cut, device):
        k = min(len(sends), send_sem.shape[0] - 1)
        return pltpu.make_async_remote_copy(
            src_ref=buf.at[pl.ds(pos[m] * rows + cut * piece, piece), pl.ds(s * depth, depth)],
            dst_ref=buf.at[pl.ds(pos[to_m] * rows + cut * piece, piece), pl.ds(to_s * depth, depth)],
            send_sem=send_sem.at[k],
            recv_sem=recv_sem.at[(to_m * n_h + to_s) * cuts + cut],
            device_id=device, device_id_type=MESH,
        )

    def send(m, s, to_m, to_s, cut, device):
        copy = block_copy(m, s, to_m, to_s, cut, device)
        copy.start()
        sends.append(copy)

    def wait_block(m, s, cut):
        if (m, s) != (0, 0):
            block_copy(m, s, m, s, cut, (flip(v, 1), z)).wait_recv()

    def arrive(g, s, cut):
        wait_block(2 * g, s, cut)
        if s + 1 < n_h and (g == 0 or via_dim(g, s + 1) is None):
            send(2 * g, s, 2 * g, s + 1, cut, (v, lax.rem(z + 1, n_h)))
        for d in dims:
            if not g & d and via_dim(g | d, s) == d:
                send(2 * g, s, 2 * (g | d), s, cut, (flip(v, 2 * d), z))
        send(2 * g, s, 2 * g + 1, s, cut, (flip(v, 1), z))

    tile = max(t for t in (512, 384, 256, 128) if cols % t == 0)

    tiles = cols // tile
    waited = set()

    def multiply(first, count, s, tile_lo, tile_hi):
        if tile_lo == tile_hi:
            return
        for g in groups[first : first + count]:
            for cut in range(cuts):
                if (g, s, cut) not in waited:
                    wait_block(2 * g + 1, s, cut)
                    waited.add((g, s, cut))
        if s not in waited:
            w_copies[s].wait()
            waited.add(s)
        k_lo = s * depth // 256 * 256
        k_hi = (s + 1) * depth // 256 * 256 if s + 1 < n_h else n_h * depth
        lo, size = first * 2 * rows, count * 2 * rows
        step = 1024 if size > 1024 and size % 1024 == 0 else size

        @pl.loop(tile_lo, tile_hi)
        def _(n):
            at = pl.ds(pl.multiple_of(n * tile, tile), tile)
            for r in range(lo, lo + size, step):
                value = jnp.dot(
                    buf[r : r + step, k_lo:k_hi], w[k_lo:k_hi, at], preferred_element_type=jnp.float32
                )
                if s == 0:
                    acc[r : r + step, at] = value
                else:
                    acc[r : r + step, at] = acc[r : r + step, at] + value

    def stats(first, count):
        half = 64

        @pl.loop(first * 2 * layers, (first + count) * 2 * layers)
        def _(p):
            label = labs[p // layers].astype(jnp.float32)
            label = jnp.transpose(jnp.broadcast_to(label, (LANES, LANES)))
            lane = lax.broadcasted_iota(jnp.int32, (half, LANES), 1) + first_col
            lane = lane.astype(jnp.float32)
            for h in range(LANES // half):
                at = pl.ds(pl.multiple_of(p * LANES + h * half, half), half)
                peak = acc[at, 0:LANES]
                for c in range(LANES, cols, LANES):
                    peak = jnp.maximum(peak, acc[at, c : c + LANES])
                here = slice(h * half, (h + 1) * half)
                part[0, here, :] = peak
                row_peak = jnp.max(peak, axis=1, keepdims=True)
                row_peak = jnp.broadcast_to(row_peak, (half, LANES))
                wanted = label[here] - lane
                total = jnp.zeros((half, LANES), jnp.float32)
                picked = jnp.zeros((half, LANES), jnp.float32)
                for c in range(0, cols, LANES):
                    x = acc[at, c : c + LANES]
                    total = total + jnp.exp(x - row_peak)
                    picked = picked + jnp.where(wanted == float(c), x, 0.0)
                part[1, here, :] = total
                part[2, here, :] = picked
            rel_stats[0, p] = jnp.max(jnp.transpose(part[0]), axis=0, keepdims=True)
            rel_stats[1, p] = jnp.sum(jnp.transpose(part[1]), axis=0, keepdims=True)
            rel_stats[2, p] = jnp.sum(jnp.transpose(part[2]), axis=0, keepdims=True)

    for cut in range(cuts):
        arrive(0, 0, cut)
    lab_copies = []
    for m in range(1, n_v):
        copy = pltpu.make_async_remote_copy(
            src_ref=lab_ref, dst_ref=labs.at[pos[m]],
            send_sem=lab_send.at[m - 1], recv_sem=lab_recv.at[m - 1],
            device_id=(flip(v, m), z), device_id_type=MESH,
        )
        copy.start()
        lab_copies.append(copy)
    labs[0] = lab_ref[...]

    all_blocks = [(g, s) for s in range(n_h) for g in groups]
    last = max(arrival(g, s) for g, s in all_blocks)
    events, jobs = {}, {}
    for t in range(last + 1):
        here = [block for block in all_blocks if arrival(*block) == t]
        events[t] = sorted(here, key=lambda block: (block[0] == 0) == (t == 2))
        ready = [(g, s) for g, s in all_blocks if t == (s + (s > 0) if g == 0 else arrival(g, s))]
        jobs[t] = []
        for g, s in ready:
            i = groups.index(g)
            if jobs[t] and jobs[t][-1][2] == s and sum(jobs[t][-1][:2]) == i:
                first, count, _ = jobs[t].pop()
                jobs[t].append((first, count + 1, s))
            else:
                jobs[t].append((i, 1, s))

    def run(t, lo, hi, of=1):
        total = sum(count for _, count, _ in jobs[t]) * tiles
        begin, end, at = total * lo // of, total * hi // of, 0
        for first, count, s in jobs[t]:
            first_tile = min(max(0, (begin - at) // count), tiles)
            last_tile = min(max(0, (end - at) // count), tiles)
            multiply(first, count, s, first_tile, last_tile)
            at += count * tiles

    early = min(first for first, _, _ in jobs[last])
    parts = cuts + 1
    for t in range(last + 1):
        for cut in range(cuts):
            if t > 0:
                for g, s in events[t]:
                    arrive(g, s, cut)
            if t > 1:
                run(t - 1, cut + 1, cut + 2, parts)
        if t == last:
            for copy in lab_copies:
                copy.wait()
            stats(0, early)
        if t in (0, last):
            run(t, 0, 1)
        else:
            run(t, 0, 1, parts)
    stats(early, len(groups) - early)

    for m in range(n_v):
        for l in range(layers):
            for k in range(3):
                line[z, pl.ds(k * blocks + flip(v, m) * layers + l, 1), :] = rel_stats[k, pos[m] * layers + l]
    line_copies = []
    for j, peer in enumerate(line_peers):
        copy = pltpu.make_async_remote_copy(
            src_ref=line.at[z], dst_ref=line.at[z],
            send_sem=line_send.at[j], recv_sem=line_recv.at[j],
            device_id=(v, peer), device_id_type=MESH,
        )
        copy.start()
        line_copies.append(copy)
    for copy in line_copies:
        copy.wait_recv()
    peak, total, picked = combine([line[h] for h in range(n_h)], blocks)
    plane[v, 0:blocks, :] = peak
    plane[v, blocks : 2 * blocks, :] = total
    plane[v, 2 * blocks : 3 * blocks, :] = picked
    plane_copies = []
    for m in range(1, n_v):
        copy = pltpu.make_async_remote_copy(
            src_ref=plane.at[v], dst_ref=plane.at[v],
            send_sem=plane_send.at[m - 1], recv_sem=plane_recv.at[m - 1],
            device_id=(flip(v, m), z), device_id_type=MESH,
        )
        copy.start()
        plane_copies.append(copy)
    for copy in sends + line_copies:
        copy.wait_send()
    for copy in plane_copies:
        copy.wait_recv()
    peak, total, picked = combine([plane[u] for u in range(n_v)], blocks)
    loss = peak + jnp.log(total) - picked
    for l in range(layers):
        sums = jnp.zeros((1, LANES), jnp.float32)
        for u in range(n_v):
            row = loss[u * layers + l : u * layers + l + 1]
            loss_ref[l : l + 1, u * LANES : (u + 1) * LANES] = row
            sums = sums + row
        mean_ref[l] = jnp.sum(sums) / (n_v * LANES)
    for copy in plane_copies:
        copy.wait_send()


def body(hidden, unembed, labels, n_v, n_h):
    layers, tokens, depth = hidden.shape
    cols = unembed.shape[1]
    rows = layers * tokens
    blocks = n_v * layers
    dma = pltpu.SemaphoreType.DMA
    any_space = pl.BlockSpec(memory_space=pl.ANY)
    vmem = pl.BlockSpec(memory_space=pltpu.VMEM)
    cuts = CUTS if n_v * n_h <= 64 else 1
    return pl.pallas_call(
        functools.partial(kernel, n_v, n_h, layers),
        out_shape=(
            jax.ShapeDtypeStruct((layers, n_v * tokens), jnp.float32),
            jax.ShapeDtypeStruct((layers,), jnp.float32),
        ),
        in_specs=[any_space, any_space, vmem],
        out_specs=(vmem, pl.BlockSpec(memory_space=pltpu.SMEM)),
        scratch_shapes=[
            pltpu.VMEM((n_v * rows, n_h * depth), jnp.bfloat16),
            pltpu.VMEM((n_h * depth, cols), jnp.bfloat16),
            pltpu.VMEM((n_v * rows, cols), jnp.float32),
            pltpu.VMEM((n_v, 1, tokens), jnp.int32),
            pltpu.VMEM((3, LANES, LANES), jnp.float32),
            pltpu.VMEM((3, blocks, 1, tokens), jnp.float32),
            pltpu.VMEM((n_h, 3 * blocks, tokens), jnp.float32),
            pltpu.VMEM((n_v, 3 * blocks, tokens), jnp.float32),
            dma,
            dma((n_h,)),
            dma(((n_v * n_h - 1) * cuts,)),
            dma((n_v * n_h * cuts,)),
            dma((n_v - 1,)),
            dma((n_v - 1,)),
            dma((n_h - 1,)),
            dma((n_h - 1,)),
            dma((n_v - 1,)),
            dma((n_v - 1,)),
        ],
        compiler_params=pltpu.CompilerParams(
            collective_id=0, has_side_effects=True, vmem_limit_bytes=60 * 2**20
        ),
    )(hidden.reshape(rows, depth), unembed, labels.reshape(1, tokens))


def solution(mesh):
    placed = (P(None, "vocab", "hid"), P(None, ("vocab", "hid")), P("vocab"))
    inner = functools.partial(body, n_v=mesh.shape["vocab"], n_h=mesh.shape["hid"])
    return jax.shard_map(inner, mesh=mesh, in_specs=placed, out_specs=(P(), P()), check_vma=False)
```

```python
import functools

import jax
import jax.numpy as jnp
from jax import lax
from jax.experimental import pallas as pl
from jax.experimental.pallas import tpu as pltpu
from jax.sharding import PartitionSpec as P

MESH = pl.DeviceIdType.MESH
LANES = 128
CUTS = 2


def bits_of(mask):
    return [1 << b for b in range(mask.bit_length()) if mask >> b & 1]


def via_dim(group, piece):
    dims = bits_of(group)
    return dims[piece] if 1 < len(dims) and piece < len(dims) else dims[0] if len(dims) == 1 else None


def arrival(group, s):
    if group == 0:
        return s
    dim = via_dim(group, s)
    if dim is None:
        return 1 + arrival(group, s - 1)
    if group == dim:
        return s + 1 if s < 2 else s + 2
    return max(3, 1 + arrival(group ^ dim, s))


def flip(index, mask):
    for bit in bits_of(mask):
        index = index + bit - 2 * bit * lax.rem(index // bit, 2)
    return index


def combine(parts, blocks):
    peaks = [part[0:blocks] for part in parts]
    peak = functools.reduce(jnp.maximum, peaks)
    total = sum(part[blocks : 2 * blocks] * jnp.exp(own - peak) for part, own in zip(parts, peaks))
    picked = sum(part[2 * blocks : 3 * blocks] for part in parts)
    return peak, total, picked


def kernel(
    n_v, n_h, layers,
    hid_hbm, w_hbm, lab_ref,
    loss_ref, mean_ref,
    buf, w, acc, labs, lanes, rel_stats, line, plane,
    own_sem, w_sem, send_sem, recv_sem, lab_send, lab_recv, line_send, line_recv, plane_send, plane_recv,
):
    v, z = lax.axis_index("vocab"), lax.axis_index("hid")
    rows = hid_hbm.shape[0]
    depth = hid_hbm.shape[1]
    cols = w_hbm.shape[1]
    first_col = (v * n_h + z) * cols
    dims = [1 << b for b in range((n_v // 2).bit_length() - 1)]
    groups = sorted(range(n_v // 2), key=lambda g: (len(bits_of(g)), g))
    pos = {2 * g + c: 2 * i + c for i, g in enumerate(groups) for c in range(2)}
    blocks = n_v * layers

    own = pltpu.make_async_copy(hid_hbm, buf.at[pl.ds(0, rows), pl.ds(0, depth)], own_sem)
    own.start()
    w_copies = []
    for s in range(n_h):
        src = lax.rem(z - s + n_h, n_h)
        copy = pltpu.make_async_copy(
            w_hbm.at[pl.ds(pl.multiple_of(src * depth, depth), depth)], w.at[pl.ds(s * depth, depth)], w_sem.at[s]
        )
        w_copies.append(copy)

    barrier = pltpu.get_barrier_semaphore()
    line_peers = [lax.rem(z + j, n_h) for j in range(1, n_h)]
    for peer in line_peers:
        pl.semaphore_signal(barrier, inc=1, device_id=(v, peer), device_id_type=MESH)
    for m in range(1, n_v):
        pl.semaphore_signal(barrier, inc=1, device_id=(flip(v, m), z), device_id_type=MESH)
    for copy in w_copies:
        copy.start()
    pl.semaphore_wait(barrier, n_h + n_v - 2)
    own.wait()

    cuts = CUTS if n_v * n_h <= 64 else 1
    piece = rows // cuts
    sends = []

    def block_copy(m, s, to_m, to_s, cut, device):
        k = min(len(sends), send_sem.shape[0] - 1)
        return pltpu.make_async_remote_copy(
            src_ref=buf.at[pl.ds(pos[m] * rows + cut * piece, piece), pl.ds(s * depth, depth)],
            dst_ref=buf.at[pl.ds(pos[to_m] * rows + cut * piece, piece), pl.ds(to_s * depth, depth)],
            send_sem=send_sem.at[k],
            recv_sem=recv_sem.at[(to_m * n_h + to_s) * cuts + cut],
            device_id=device, device_id_type=MESH,
        )

    def send(m, s, to_m, to_s, cut, device):
        copy = block_copy(m, s, to_m, to_s, cut, device)
        copy.start()
        sends.append(copy)

    def wait_block(m, s, cut):
        if (m, s) != (0, 0):
            block_copy(m, s, m, s, cut, (flip(v, 1), z)).wait_recv()

    def arrive(g, s, cut):
        wait_block(2 * g, s, cut)
        if s + 1 < n_h and (g == 0 or via_dim(g, s + 1) is None):
            send(2 * g, s, 2 * g, s + 1, cut, (v, lax.rem(z + 1, n_h)))
        for d in dims:
            if not g & d and via_dim(g | d, s) == d:
                send(2 * g, s, 2 * (g | d), s, cut, (flip(v, 2 * d), z))
        send(2 * g, s, 2 * g + 1, s, cut, (flip(v, 1), z))

    tile = max(t for t in (512, 384, 256, 128) if cols % t == 0)

    tiles = cols // tile
    waited = set()

    def multiply(first, count, s, tile_lo, tile_hi):
        if tile_lo == tile_hi:
            return
        for g in groups[first : first + count]:
            for cut in range(cuts):
                if (g, s, cut) not in waited:
                    wait_block(2 * g + 1, s, cut)
                    waited.add((g, s, cut))
        if s not in waited:
            w_copies[s].wait()
            waited.add(s)
        k_lo = s * depth // 256 * 256
        k_hi = (s + 1) * depth // 256 * 256 if s + 1 < n_h else n_h * depth
        lo, size = first * 2 * rows, count * 2 * rows
        step = 1024 if size > 1024 and size % 1024 == 0 else size

        @pl.loop(tile_lo, tile_hi)
        def _(n):
            at = pl.ds(pl.multiple_of(n * tile, tile), tile)
            for r in range(lo, lo + size, step):
                value = jnp.dot(
                    buf[r : r + step, k_lo:k_hi], w[k_lo:k_hi, at], preferred_element_type=jnp.float32
                )
                if s > 0:
                    value = acc[r : r + step, at] + value
                if s + 1 < n_h:
                    acc[r : r + step, at] = value
                    continue
                here = slice(r, r + step)
                chunks = [value[:, c : c + LANES] for c in range(0, tile, LANES)]
                old = lanes[0, here, :]
                peak = functools.reduce(jnp.maximum, chunks, old)
                total = lanes[1, here, :] * jnp.exp(old - peak)
                picked = lanes[2, here, :]
                wanted = lanes[3, here, :] - (n * tile).astype(jnp.float32)
                for i, x in enumerate(chunks):
                    total = total + jnp.exp(x - peak)
                    picked = picked + jnp.where(wanted == float(i * LANES), x, 0.0)
                lanes[0, here, :] = peak
                lanes[1, here, :] = total
                lanes[2, here, :] = picked

    def prepare():
        for copy in lab_copies:
            copy.wait()
        lane = (lax.broadcasted_iota(jnp.int32, (LANES, LANES), 1) + first_col).astype(jnp.float32)

        @pl.loop(0, blocks)
        def _(p):
            at = pl.ds(pl.multiple_of(p * LANES, LANES), LANES)
            label = jnp.broadcast_to(labs[p // layers].astype(jnp.float32), (LANES, LANES))
            lanes[0, at, :] = jnp.full((LANES, LANES), -jnp.inf, jnp.float32)
            lanes[1, at, :] = jnp.zeros((LANES, LANES), jnp.float32)
            lanes[2, at, :] = jnp.zeros((LANES, LANES), jnp.float32)
            lanes[3, at, :] = jnp.transpose(label) - lane

    def stats(first, count):
        @pl.loop(first * 2 * layers, (first + count) * 2 * layers)
        def _(p):
            at = pl.ds(pl.multiple_of(p * LANES, LANES), LANES)
            peak = jnp.transpose(lanes[0, at, :])
            row_peak = jnp.max(peak, axis=0, keepdims=True)
            total = jnp.transpose(lanes[1, at, :]) * jnp.exp(peak - row_peak)
            rel_stats[0, p] = row_peak
            rel_stats[1, p] = jnp.sum(total, axis=0, keepdims=True)
            rel_stats[2, p] = jnp.sum(jnp.transpose(lanes[2, at, :]), axis=0, keepdims=True)

    for cut in range(cuts):
        arrive(0, 0, cut)
    lab_copies = []
    for m in range(1, n_v):
        copy = pltpu.make_async_remote_copy(
            src_ref=lab_ref, dst_ref=labs.at[pos[m]],
            send_sem=lab_send.at[m - 1], recv_sem=lab_recv.at[m - 1],
            device_id=(flip(v, m), z), device_id_type=MESH,
        )
        copy.start()
        lab_copies.append(copy)
    labs[0] = lab_ref[...]

    all_blocks = [(g, s) for s in range(n_h) for g in groups]
    last = max(arrival(g, s) for g, s in all_blocks)
    events, jobs = {}, {}
    for t in range(last + 1):
        here = [block for block in all_blocks if arrival(*block) == t]
        events[t] = sorted(here, key=lambda block: (block[0] == 0) == (t == 2))
        ready = [(g, s) for g, s in all_blocks if t == (s + (s > 0) if g == 0 else arrival(g, s))]
        jobs[t] = []
        for g, s in ready:
            i = groups.index(g)
            if jobs[t] and jobs[t][-1][2] == s and sum(jobs[t][-1][:2]) == i:
                first, count, _ = jobs[t].pop()
                jobs[t].append((first, count + 1, s))
            else:
                jobs[t].append((i, 1, s))

    def run(t, lo, hi, of=1):
        total = sum(count for _, count, _ in jobs[t]) * tiles
        begin, end, at = total * lo // of, total * hi // of, 0
        for first, count, s in jobs[t]:
            first_tile = min(max(0, (begin - at) // count), tiles)
            last_tile = min(max(0, (end - at) // count), tiles)
            multiply(first, count, s, first_tile, last_tile)
            at += count * tiles

    early = min(first for first, _, _ in jobs[last])
    parts = cuts + 1
    for t in range(last + 1):
        if t == min(2, last):
            prepare()
        for cut in range(cuts):
            if t > 0:
                for g, s in events[t]:
                    arrive(g, s, cut)
            if t > 1:
                run(t - 1, cut + 1, cut + 2, parts)
        if t == last:
            stats(0, early)
        if t in (0, last):
            run(t, 0, 1)
        else:
            run(t, 0, 1, parts)
    stats(early, len(groups) - early)

    for m in range(n_v):
        for l in range(layers):
            for k in range(3):
                line[z, pl.ds(k * blocks + flip(v, m) * layers + l, 1), :] = rel_stats[k, pos[m] * layers + l]
    line_copies = []
    for j, peer in enumerate(line_peers):
        copy = pltpu.make_async_remote_copy(
            src_ref=line.at[z], dst_ref=line.at[z],
            send_sem=line_send.at[j], recv_sem=line_recv.at[j],
            device_id=(v, peer), device_id_type=MESH,
        )
        copy.start()
        line_copies.append(copy)
    for copy in line_copies:
        copy.wait_recv()
    peak, total, picked = combine([line[h] for h in range(n_h)], blocks)
    plane[v, 0:blocks, :] = peak
    plane[v, blocks : 2 * blocks, :] = total
    plane[v, 2 * blocks : 3 * blocks, :] = picked
    plane_copies = []
    for m in range(1, n_v):
        copy = pltpu.make_async_remote_copy(
            src_ref=plane.at[v], dst_ref=plane.at[v],
            send_sem=plane_send.at[m - 1], recv_sem=plane_recv.at[m - 1],
            device_id=(flip(v, m), z), device_id_type=MESH,
        )
        copy.start()
        plane_copies.append(copy)
    for copy in sends + line_copies:
        copy.wait_send()
    for copy in plane_copies:
        copy.wait_recv()
    peak, total, picked = combine([plane[u] for u in range(n_v)], blocks)
    loss = peak + jnp.log(total) - picked
    for l in range(layers):
        sums = jnp.zeros((1, LANES), jnp.float32)
        for u in range(n_v):
            row = loss[u * layers + l : u * layers + l + 1]
            loss_ref[l : l + 1, u * LANES : (u + 1) * LANES] = row
            sums = sums + row
        mean_ref[l] = jnp.sum(sums) / (n_v * LANES)
    for copy in plane_copies:
        copy.wait_send()


def body(hidden, unembed, labels, n_v, n_h):
    layers, tokens, depth = hidden.shape
    cols = unembed.shape[1]
    rows = layers * tokens
    blocks = n_v * layers
    dma = pltpu.SemaphoreType.DMA
    any_space = pl.BlockSpec(memory_space=pl.ANY)
    vmem = pl.BlockSpec(memory_space=pltpu.VMEM)
    cuts = CUTS if n_v * n_h <= 64 else 1
    return pl.pallas_call(
        functools.partial(kernel, n_v, n_h, layers),
        out_shape=(
            jax.ShapeDtypeStruct((layers, n_v * tokens), jnp.float32),
            jax.ShapeDtypeStruct((layers,), jnp.float32),
        ),
        in_specs=[any_space, any_space, vmem],
        out_specs=(vmem, pl.BlockSpec(memory_space=pltpu.SMEM)),
        scratch_shapes=[
            pltpu.VMEM((n_v * rows, n_h * depth), jnp.bfloat16),
            pltpu.VMEM((n_h * depth, cols), jnp.bfloat16),
            pltpu.VMEM((n_v * rows, cols), jnp.float32),
            pltpu.VMEM((n_v, 1, tokens), jnp.int32),
            pltpu.VMEM((4, n_v * rows, LANES), jnp.float32),
            pltpu.VMEM((3, blocks, 1, tokens), jnp.float32),
            pltpu.VMEM((n_h, 3 * blocks, tokens), jnp.float32),
            pltpu.VMEM((n_v, 3 * blocks, tokens), jnp.float32),
            dma,
            dma((n_h,)),
            dma(((n_v * n_h - 1) * cuts,)),
            dma((n_v * n_h * cuts,)),
            dma((n_v - 1,)),
            dma((n_v - 1,)),
            dma((n_h - 1,)),
            dma((n_h - 1,)),
            dma((n_v - 1,)),
            dma((n_v - 1,)),
        ],
        compiler_params=pltpu.CompilerParams(
            collective_id=0, has_side_effects=True, vmem_limit_bytes=60 * 2**20
        ),
    )(hidden.reshape(rows, depth), unembed, labels.reshape(1, tokens))


def solution(mesh):
    placed = (P(None, "vocab", "hid"), P(None, ("vocab", "hid")), P("vocab"))
    inner = functools.partial(body, n_v=mesh.shape["vocab"], n_h=mesh.shape["hid"])
    return jax.shard_map(inner, mesh=mesh, in_specs=placed, out_specs=(P(), P()), check_vma=False)
```
